32 devices in a mesh: ctx: 16 (over z, x, core), head: 2 (over y).
Axes of the slice: x: 2, y: 2, z: 4, core: 2. Of those that a mesh axis runs over, the one named last changes fastest.
Arguments:
- teacher_queries: bfloat16 [8192, 4096], P('ctx', 'head'), may hold values from -13.5 to 13.5
- teacher_keys: bfloat16 [8192, 1024], P('ctx', 'head'), may hold values from -6 to 6
- query_projection: float32 [32, 128, 128], P('head'), may hold values from -0.5 to 0.5
- key_projection: float32 [8, 384, 128], P('head'), may hold values from -0.3125 to 0.3125
- block_offsets: int32 [128, 24], P('ctx'), may hold values from 0 to 24, as said below
- valid_counts: int32 [128], P('ctx'), may hold values from 1 to 24, as said below
Outputs:
- query_gradient: float32 [32, 128, 128], P('head')
- key_gradient: float32 [8, 384, 128], P('head')
- mean_divergence: float32 [], replicated
The draws below stay inside these ranges and needn't reach their ends.
Inputs may be any that keep to these rules, and one draw needn't show every extreme that they name: `block_offsets`: each row holds distinct offsets, the first of them 0 (a block's own diagonal block); the largest offset is reached in every draw. `valid_counts`: both ends are reached in every draw.
All inputs are finite; a program needn't handle non-finite values.
Results may differ from the reference program's by a relative error of at most 0.0003.
Values may be sent and summed in bfloat16 or wider, within the bound.
A program may use at most 64 MiB of HBM per device.

```python
import math
import jax
import jax.numpy as jnp
from jax import lax

HEADS = 32
KV_HEADS = 8
HEAD_DIM = 128
GATE_WIDTH = 128
BLOCK = 64
CAND = 24
REACH = 4
QB_DEV = 8
TOKENS = 8192
QBLOCKS = 128
N_CTX = 16


def paired_draw(key):
    base = jax.random.fold_in(key, 11)
    group_size = HEADS // KV_HEADS
    keys_float = jax.random.normal(jax.random.fold_in(base, 1), (TOKENS, KV_HEADS, HEAD_DIM), jnp.float32)
    queries_float = jax.random.normal(jax.random.fold_in(base, 2), (TOKENS, KV_HEADS, group_size, HEAD_DIM), jnp.float32)
    keys_float = jnp.clip(keys_float, -6.0, 6.0)
    queries_float = jnp.clip(queries_float, -6.0, 6.0)
    return (queries_float.reshape(TOKENS, HEADS * HEAD_DIM), keys_float.reshape(TOKENS, KV_HEADS * HEAD_DIM))


def draw_teacher_queries(key, part):
    return paired_draw(key)[0].astype(jnp.bfloat16)


def draw_teacher_keys(key, part):
    return paired_draw(key)[1].astype(jnp.bfloat16)


def draw_block_offsets(key, part):
    span_max = (REACH - 1) * QB_DEV
    row_keys = jax.random.split(jax.random.fold_in(key, 21), QBLOCKS)
    orders = jax.vmap(lambda one_key: jax.random.permutation(one_key, span_max) + 1)(row_keys)
    picked = orders[:, :CAND - 1].astype(jnp.int32)
    row_index = jnp.arange(QBLOCKS)
    needed = (row_index % QB_DEV == 0) & jnp.logical_not(jnp.any(picked == span_max, axis=1))
    last_slot = jnp.where(needed, span_max, picked[:, CAND - 2]).astype(jnp.int32)
    zeros_col = jnp.zeros((QBLOCKS, 1), jnp.int32)
    return jnp.concatenate([zeros_col, picked[:, :CAND - 2], last_slot[:, None]], axis=1).astype(jnp.int32)


def draw_valid_counts(key, part):
    counts = jax.random.randint(jax.random.fold_in(key, 31), (QBLOCKS,), 1, CAND + 1)
    row_index = jnp.arange(QBLOCKS)
    counts = jnp.where(row_index % QB_DEV == 0, CAND, counts)
    counts = jnp.where(row_index % QB_DEV == 1, 1, counts)
    return counts.astype(jnp.int32)


def block_levels(rng, dims, pieces, low, high):
    loudness = 1.0
    for dim, shards_of in pieces:
        steps = jax.random.uniform(jax.random.fold_in(jax.random.fold_in(rng, 6), dim), (shards_of,), jnp.float32, low / len(pieces), high / len(pieces))
        loudness = loudness * jnp.repeat(jnp.exp(steps), dims[dim] // shards_of).reshape((-1,) + (1,) * (len(dims) - 1 - dim))
    return loudness


def gaussian(key, shape, scale, bound, pieces=(), kind=jnp.bfloat16):
    array = scale * jax.random.normal(key, shape, jnp.float32)
    if pieces:
        array = array * block_levels(key, shape, pieces, -0.22, 0.18)
    return jnp.clip(array, -bound, bound).astype(kind)


def setup_inputs(seed: int = 0) -> dict:
    arg_keys = jax.random.split(jax.random.key(seed), 7)
    teacher_queries = draw_teacher_queries(jax.random.fold_in(arg_keys[6], 71), 0)
    teacher_keys = draw_teacher_keys(jax.random.fold_in(arg_keys[6], 71), 0)
    query_projection = gaussian(arg_keys[2], (HEADS, HEAD_DIM, GATE_WIDTH), HEAD_DIM ** -0.5, 0.5, ((0, 2),), jnp.float32)
    key_projection = gaussian(arg_keys[3], (KV_HEADS, 3 * HEAD_DIM, GATE_WIDTH), (3 * HEAD_DIM) ** -0.5, 0.3125, ((0, 2),), jnp.float32)
    block_offsets = draw_block_offsets(jax.random.fold_in(arg_keys[6], 71), 0)
    valid_counts = draw_valid_counts(jax.random.fold_in(arg_keys[6], 71), 0)
    return dict(teacher_queries=teacher_queries, teacher_keys=teacher_keys, query_projection=query_projection, key_projection=key_projection, block_offsets=block_offsets, valid_counts=valid_counts)


def block_map(query_block, cand_keys, offsets, usable):
    scores = jnp.einsum('tgrd,cugd->grtcu', query_block, cand_keys, preferred_element_type=jnp.float32) / math.sqrt(query_block.shape[-1])
    width = query_block.shape[0]
    query_pos = jnp.arange(width)[:, None, None]
    key_pos = jnp.arange(width)[None, None, :]
    allowed = ((offsets[None, :, None] != 0) | (key_pos <= query_pos)) & usable[None, :, None]
    scores = jnp.where(allowed, scores, -jnp.inf)
    top_score = lax.optimization_barrier(jnp.max(scores, axis=(3, 4), keepdims=True))
    weights = jnp.exp(scores - top_score)
    per_block = lax.optimization_barrier(jnp.sum(weights, axis=4))
    shares = per_block / lax.optimization_barrier(jnp.sum(per_block, axis=3, keepdims=True))
    return lax.optimization_barrier(jnp.mean(shares, axis=2))

def gate_terms(gate_query, cand_gate, teacher_map, usable):
    logits = jnp.einsum('bgre,bcge->bgrc', gate_query, cand_gate, precision=lax.Precision.HIGHEST) / math.sqrt(gate_query.shape[-1])
    mask = usable[:, None, None, :]
    logits = jnp.where(mask, logits, -jnp.inf)
    log_gate = logits - jax.nn.logsumexp(logits, axis=3, keepdims=True)
    log_gate = jnp.where(mask, log_gate, 0.0)
    terms = jnp.where(mask, jax.scipy.special.xlogy(teacher_map, teacher_map) - teacher_map * log_gate, 0.0)
    return jnp.sum(terms)

def reference(teacher_queries, teacher_keys, query_projection, key_projection, block_offsets, valid_counts):
    group_size = HEADS // KV_HEADS
    query_blocks = teacher_queries.reshape(QBLOCKS, BLOCK, KV_HEADS, group_size, HEAD_DIM)
    key_blocks = teacher_keys.reshape(QBLOCKS, BLOCK, KV_HEADS, HEAD_DIM)
    row_index = jnp.arange(QBLOCKS, dtype=jnp.int32)
    key_block = row_index[:, None] - block_offsets
    slot_index = jnp.arange(CAND, dtype=jnp.int32)
    usable = (slot_index[None, :] < valid_counts[:, None]) & (key_block >= 0)
    cand_index = jnp.maximum(key_block, 0).astype(jnp.int32)

    def one_block(inputs):
        query_block, index_row, offsets, usable_row = inputs
        cand_keys = key_blocks[index_row]
        return block_map(query_block.astype(jnp.float32), cand_keys.astype(jnp.float32), offsets, usable_row)
    teacher_map = lax.map(one_block, (query_blocks, cand_index, block_offsets, usable))
    pooled_query = lax.optimization_barrier(jnp.mean(query_blocks.astype(jnp.float32), axis=1))
    keys_float = key_blocks.astype(jnp.float32)
    pooled_key = jnp.concatenate([lax.optimization_barrier(jnp.max(keys_float, axis=1)), lax.optimization_barrier(jnp.min(keys_float, axis=1)), lax.optimization_barrier(jnp.mean(keys_float, axis=1))], axis=-1)

    def total_loss(query_weights, key_weights):
        gate_query = jnp.einsum('bgrd,grde->bgre', pooled_query, query_weights.reshape(KV_HEADS, group_size, HEAD_DIM, GATE_WIDTH), precision=lax.Precision.HIGHEST)
        gate_key = jnp.einsum('ngf,gfe->nge', pooled_key, key_weights, precision=lax.Precision.HIGHEST)
        shaped = (N_CTX, QB_DEV)

        def one_shard(inputs):
            shard_query, shard_index, shard_map, shard_usable = inputs
            return gate_terms(shard_query, gate_key[shard_index], shard_map, shard_usable)
        parts = lax.map(one_shard, (gate_query.reshape(shaped + gate_query.shape[1:]), cand_index.reshape(shaped + (CAND,)), teacher_map.reshape(shaped + teacher_map.shape[1:]), usable.reshape(shaped + (CAND,))))
        return jnp.sum(parts)
    kl_total, grads = jax.value_and_grad(total_loss, argnums=(0, 1))(query_projection, key_projection)
    grad_scale = 1.0 / math.sqrt(QBLOCKS)
    return (grads[0] * grad_scale, grads[1] * grad_scale, kl_total / (QBLOCKS * HEADS))
```

```python
import functools
import math

import jax
import jax.numpy as jnp
from jax import lax
from jax.experimental import pallas as pl
from jax.experimental.pallas import tpu as pltpu
from jax.sharding import PartitionSpec as P

HEAD_DIM = 128
BLOCK = 64
REACH = 4
PIECES = 2
MESH = pl.DeviceIdType.MESH
F32 = jnp.float32
BF16 = jnp.bfloat16
LOW = -3.0e38
NT = (((1,), (1,)), ((), ()))
NN = (((1,), (0,)), ((), ()))
TN = (((0,), (0,)), ((), ()))


def exact(a, b, dims):
    return lax.dot_general(
        a, b, dims, precision=lax.Precision.HIGHEST, preferred_element_type=F32
    )


def halves(a):
    high = a.astype(BF16)
    return high, (a - high.astype(F32)).astype(BF16)


def dot3(a, b, dims):
    ah, al = halves(a)
    bh, bl = halves(b)
    one = functools.partial(
        lax.dot_general, dimension_numbers=dims, preferred_element_type=F32
    )
    return one(ah, bh) + (one(ah, bl) + one(al, bh))


def flipped(me, mask):
    out = me
    bit = 0
    while mask >> bit:
        if (mask >> bit) & 1:
            size = 1 << bit
            out = out + size - 2 * size * ((me // size) % 2)
        bit += 1
    return out


class Spread:
    def __init__(self, me, count, buf, send, recv):
        self.me, self.buf, self.send, self.recv = me, buf, send, recv
        self.bits = count.bit_length() - 1
        self.index = {}
        for bit in reversed(range(self.bits)):
            for high in range(1 << (self.bits - 1 - bit)):
                self.index[bit, high] = len(self.index)
        self.order = sorted(
            self.index, key=lambda key: (bin(key[1]).count("1"), -key[0])
        )
        self.done = 0

    def copy(self, bit, high):
        at = self.index[bit, high]
        slot = flipped(self.me, high << (bit + 1))
        return pltpu.make_async_remote_copy(
            src_ref=self.buf.at[slot],
            dst_ref=self.buf.at[slot],
            send_sem=self.send.at[at],
            recv_sem=self.recv.at[at],
            device_id={"ctx": flipped(self.me, 1 << bit)},
            device_id_type=MESH,
        )

    def start(self):
        for bit in reversed(range(self.bits)):
            self.copy(bit, 0).start()

    def forward(self, steps):
        for bit, high in self.order[self.done : self.done + steps]:
            self.copy(bit, high).wait_recv()
            held = (1 << bit) | (high << (bit + 1))
            for lower in reversed(range(bit)):
                self.copy(lower, held >> (lower + 1)).start()
        self.done += steps

    def finish(self):
        self.forward(len(self.order) - self.done)
        for bit, high in self.order:
            self.copy(bit, high).wait_send()


def kernel(
    count,
    heads_axis,
    q_in,
    k_in,
    wq_in,
    wk_in,
    off_in,
    cnt_in,
    early,
    dq_all,
    dk_pad,
    total_out,
    q_ref,
    k_ref,
    wq_ref,
    wk_ref,
    off_ref,
    cnt_ref,
    load,
    win,
    late,
    peer,
    top,
    mass,
    mask,
    tmap,
    gq_own,
    gq_all,
    gk_pad,
    win_send,
    win_recv,
    early_send,
    early_recv,
    late_send,
    late_recv,
    peer_send,
    peer_recv,
):
    loads = [
        pltpu.make_async_copy(src, dst, load.at[at])
        for at, (src, dst) in enumerate(
            (
                (k_in, k_ref),
                (q_in, q_ref),
                (off_in, off_ref),
                (cnt_in, cnt_ref),
                (wq_in, wq_ref),
                (wk_in, wk_ref),
            )
        )
    ]
    for copy in loads:
        copy.start()
    me = lax.axis_index("ctx")
    side = lax.axis_index("head")
    rows, width = q_ref.shape
    here = rows // BLOCK
    heads = width // HEAD_DIM
    kv = k_ref.shape[1] // HEAD_DIM
    group = heads // kv
    slots = off_ref.shape[1]
    blocks = REACH * here
    past = (REACH - 1) * here
    lanes = heads * here
    bits = count.bit_length() - 1
    span = group * BLOCK

    piece = rows // PIECES
    odd = lax.rem(me, 2) == 1

    def window_copy(kind, at, relay, step, target):
        base = (REACH - 3) * rows + at * piece
        dst = pl.ds((REACH - 1 - step) * rows + at * piece, piece)
        src = win.at[pl.ds(base, piece)] if relay else k_in.at[pl.ds(at * piece, piece)]
        return pltpu.make_async_remote_copy(
            src_ref=src,
            dst_ref=win.at[dst],
            send_sem=win_send.at[kind, at],
            recv_sem=win_recv.at[step - 1, at],
            device_id={"ctx": lax.rem(target + count, count)},
            device_id_type=MESH,
        )

    def chip_copies(at):
        return (
            (me + 2 < count, window_copy(0, at, False, 2, me + 2)),
            (jnp.logical_not(odd), window_copy(1, at, False, 1, me + 1)),
        )

    def relay_copies(at):
        return (
            (odd & (me >= 2) & (me + 1 < count), window_copy(2, at, True, 3, me + 1)),
            (jnp.logical_not(odd) & (me >= 2), window_copy(3, at, True, 3, me + 1)),
            (odd & (me >= 2), window_copy(4, at, True, 1, me - 1)),
        )

    def arrived(step, at):
        return window_copy(0, at, False, step, me + 2).wait_recv()

    def relay(at):
        @pl.when(me >= 2)
        def _():
            arrived(2, at)

        for condition, copy in relay_copies(at):
            pl.when(condition)(copy.start)

    barrier = pltpu.get_barrier_semaphore()
    greeted = 0
    for step in range(1, REACH):
        for other in (lax.rem(me + step, count), lax.rem(me + count - step, count)):
            pl.semaphore_signal(
                barrier, inc=1, device_id={"ctx": other}, device_id_type=MESH
            )
            greeted += 1
    for bit in range(bits):
        pl.semaphore_signal(
            barrier, inc=1, device_id={"ctx": flipped(me, 1 << bit)}, device_id_type=MESH
        )
        greeted += 1
    for step in range(1, heads_axis):
        pl.semaphore_signal(
            barrier,
            inc=1,
            device_id={"head": lax.rem(side + step, heads_axis)},
            device_id_type=MESH,
        )
        greeted += 1
    pl.semaphore_wait(barrier, greeted)

    for at in range(PIECES):
        for condition, copy in chip_copies(at):
            pl.when(condition)(copy.start)

    for step in range(1, REACH):

        @pl.when(me < step)
        def _():
            win[(REACH - 1 - step) * rows : (REACH - step) * rows, :] = jnp.zeros(
                k_ref.shape, k_ref.dtype
            )

    for copy in loads[:4]:
        copy.wait()

    pool_row = lax.broadcasted_iota(jnp.int32, (here, rows), 0)
    pool_col = lax.broadcasted_iota(jnp.int32, (here, rows), 1)
    pool = jnp.where(pool_col // BLOCK == pool_row, 1.0 / BLOCK, 0.0).astype(BF16)
    for h in range(heads):
        early[me, h * here : (h + 1) * here, :] = lax.dot_general(
            pool,
            q_ref[:, h * HEAD_DIM : (h + 1) * HEAD_DIM],
            NN,
            preferred_element_type=F32,
        )
    for g in range(kv):
        keys = k_ref[:, g * HEAD_DIM : (g + 1) * HEAD_DIM]
        split = keys.astype(F32).reshape(here, BLOCK, HEAD_DIM)
        mean = lax.dot_general(pool, keys, NN, preferred_element_type=F32)
        for part, value in enumerate((jnp.max(split, axis=1), jnp.min(split, axis=1), mean)):
            at = lanes + (g * 3 + part) * here
            early[me, at : at + here, :] = value
    first = Spread(me, count, early, early_send, early_recv)
    first.start()

    row_w = lax.broadcasted_iota(jnp.int32, (blocks, 128), 0)
    for j in range(here):
        back = past + j - row_w
        used = jnp.zeros((blocks, 128), F32)
        for c in range(slots):
            off = jnp.where(c < cnt_ref[0, j], off_ref[j, c], -1000)
            used = jnp.where(back == off, 1.0, used)
        mask[j] = jnp.where(row_w >= past - me * here, used, 0.0)

    log_scale = math.log2(math.e) / math.sqrt(HEAD_DIM)
    gap = lax.broadcasted_iota(jnp.int32, (BLOCK, span), 0) - (
        lax.broadcasted_iota(jnp.int32, (BLOCK, span), 1) % BLOCK
    )

    def section(base, keys_ref, key_row, diagonal):
        def one(j, carry):
            at = pl.ds(pl.multiple_of(j * BLOCK, BLOCK), BLOCK)
            for g in range(kv):
                queries = jnp.concatenate(
                    [
                        q_ref[at, (g * group + r) * HEAD_DIM : (g * group + r + 1) * HEAD_DIM]
                        for r in range(group)
                    ],
                    axis=0,
                )
                keys = keys_ref[pl.ds(key_row, rows), g * HEAD_DIM : (g + 1) * HEAD_DIM]
                scores = lax.dot_general(keys, queries, NT, preferred_element_type=F32)
                tops, sums = [], []
                for w in range(here):
                    part = scores[w * BLOCK : (w + 1) * BLOCK]
                    if diagonal:
                        part = jnp.where(gap <= jnp.where(j == w, 0, BLOCK), part, LOW)
                    high = jnp.max(part, axis=0, keepdims=True)
                    tops.append(high)
                    sums.append(
                        jnp.sum(jnp.exp2((part - high) * log_scale), axis=0, keepdims=True)
                    )
                top[j * kv + g, pl.ds(base, here), :] = jnp.concatenate(tops, axis=0)
                mass[j * kv + g, pl.ds(base, here), :] = jnp.concatenate(sums, axis=0)
            return carry

        lax.fori_loop(0, here, one, 0)

    def reached(step):
        @pl.when(me >= step)
        def _():
            for at in range(PIECES):
                arrived(step, at)

    def window_section(step):
        slot = REACH - 1 - step
        section(
            pl.multiple_of(slot * here, here), win, pl.multiple_of(slot * rows, rows), False
        )

    section(past, k_ref, 0, True)
    loads[4].wait()
    loads[5].wait()
    relay(0)
    own_gq = jnp.concatenate(
        [
            exact(early[me, h * here : (h + 1) * here, :], wq_ref[h], NN)
            for h in range(heads)
        ],
        axis=0,
    )
    gq_own[...] = own_gq
    for at in range(1, PIECES):
        relay(at)

    @pl.when(odd)
    def _():
        reached(1)

    window_section(jnp.where(odd, 1, 2))
    first.forward(min(3, len(first.order)))

    @pl.when(jnp.logical_not(odd))
    def _():
        reached(1)

    window_section(jnp.where(odd, 2, 1))
    first.forward(min(4, len(first.order) - first.done))
    reached(3)
    window_section(3)

    spread_row = lax.broadcasted_iota(jnp.int32, (span, 128), 0)
    spread_col = lax.broadcasted_iota(jnp.int32, (span, 128), 1)
    spread = jnp.where(spread_col == (spread_row // BLOCK) * here, 1.0 / BLOCK, 0.0).astype(BF16)
    tmap[...] = jnp.zeros(tmap.shape, F32)

    def combine(j, carry):
        used = mask[j] > 0.5
        used = jnp.concatenate([used] * (span // 128), axis=1)
        for g in range(kv):
            high = jnp.where(used, top[j * kv + g], LOW)
            best = jnp.max(high, axis=0, keepdims=True)
            share = jnp.where(used, mass[j * kv + g], 0.0) * jnp.exp2((high - best) * log_scale)
            share = share / jnp.sum(share, axis=0, keepdims=True)
            sh, sl = halves(share)
            mean = lax.dot_general(sh, spread, NN, preferred_element_type=F32)
            mean = mean + lax.dot_general(sl, spread, NN, preferred_element_type=F32)
            tmap[...] += pltpu.roll(mean, g * group * here + j, axis=1)
        return carry

    lax.fori_loop(0, here, combine, 0)

    first.forward(len(first.order) - first.done)

    gk_pad[:, :past, :] = jnp.zeros((kv, past, HEAD_DIM), F32)
    dk_pad[...] = jnp.zeros(dk_pad.shape, F32)

    def pooled_keys(g, part):
        at = lanes + (g * 3 + part) * here
        return early[:, at : at + here, :].reshape(count * here, HEAD_DIM)

    for g in range(kv):
        acc = exact(pooled_keys(g, 0), wk_ref[g, :HEAD_DIM, :], NN)
        for part in range(1, 3):
            acc = acc + exact(
                pooled_keys(g, part), wk_ref[g, part * HEAD_DIM : (part + 1) * HEAD_DIM, :], NN
            )
        gk_pad[g, past:, :] = acc

    def window_keys(s):
        at = pl.ds(pl.multiple_of(s * here, here), blocks)
        return jnp.concatenate([gk_pad[g, at, :] for g in range(kv)], axis=0)

    lane = lax.broadcasted_iota(jnp.int32, (blocks, lanes), 1)
    lane_group = lane // (group * here)
    full = exact(window_keys(me), gq_own[...], NT)
    logits = jnp.zeros((blocks, lanes), F32)
    used = jnp.zeros((blocks, lanes), F32)
    for g in range(kv):
        logits = jnp.where(lane_group == g, full[g * blocks : (g + 1) * blocks], logits)
    for j in range(here):
        used = jnp.where(lane % here == j, mask[j], used)
    used = used > 0.5
    logits = jnp.where(used, logits / math.sqrt(HEAD_DIM), LOW)
    logits = logits - jnp.max(logits, axis=0, keepdims=True)
    weights = jnp.where(used, jnp.exp(logits), 0.0)
    norm = jnp.sum(weights, axis=0, keepdims=True)
    log_gate = jnp.where(used, logits - jnp.log(norm), 0.0)
    teacher = jnp.where(used, tmap[...], 0.0)
    log_teacher = jnp.log(jnp.where(teacher > 0.0, teacher, 1.0))
    terms = teacher * (log_teacher - log_gate)
    block_total = count * here
    scale = 1.0 / (math.sqrt(block_total) * math.sqrt(HEAD_DIM))
    slope = jnp.sum(teacher, axis=0, keepdims=True) * (weights / norm) - teacher
    late[me, :blocks, :] = jnp.where(used, slope, 0.0) * scale
    part = terms[:8]
    for at in range(8, blocks, 8):
        part = part + terms[at : at + 8]
    late[me, blocks : blocks + 8, :] = part
    second = Spread(me, count, late, late_send, late_recv)
    second.start()

    for h in range(heads):
        pooled = early[:, h * here : (h + 1) * here, :].reshape(count * here, HEAD_DIM)
        gq_all[:, h * here : (h + 1) * here, :] = dot3(pooled, wq_ref[h], NN).reshape(
            count, here, HEAD_DIM
        )
        if h >= heads // 4:
            second.forward(min(1, len(second.order) - second.done))
    second.forward(len(second.order) - second.done)

    total = late[0, blocks : blocks + 8, :]
    for s in range(1, count):
        total = total + late[s, blocks : blocks + 8, :]
    peer[side] = total

    def peer_copy(step):
        return pltpu.make_async_remote_copy(
            src_ref=peer.at[side],
            dst_ref=peer.at[side],
            send_sem=peer_send.at[step - 1],
            recv_sem=peer_recv.at[step - 1],
            device_id={"head": lax.rem(side + step, heads_axis)},
            device_id_type=MESH,
        )

    for step in range(1, heads_axis):
        peer_copy(step).start()

    def backward(s, carry):
        slope = late[s, :blocks, :]
        banded = jnp.concatenate(
            [jnp.where(lane_group == g, slope, 0.0) for g in range(kv)], axis=0
        )
        dq_all[s] = dot3(banded, window_keys(s), TN)
        dk = dot3(banded, gq_all[s], NN)
        at = pl.ds(pl.multiple_of(s * here, here), blocks)
        for g in range(kv):
            dk_pad[g, at, :] += dk[g * blocks : (g + 1) * blocks]
        return carry

    lax.fori_loop(0, count, backward, 0)
    for step in range(1, heads_axis):
        peer_copy(step).wait_recv()
    total = peer[0]
    for step in range(1, heads_axis):
        total = total + peer[step]
    total = jnp.sum(jnp.sum(total, axis=0, keepdims=True), axis=1, keepdims=True)
    total_out[...] = total / (block_total * heads * heads_axis)
    for step in range(1, heads_axis):
        peer_copy(step).wait_send()
    first.finish()
    second.finish()
    for at in range(PIECES):
        for condition, copy in chip_copies(at) + relay_copies(at):
            pl.when(condition)(copy.wait_send)


def finish(early, dq_all, dk_pad, gq_hbm, gk_hbm, gq_buf, gk_buf, sems):
    count = early.shape[0]
    heads, kv = gq_buf.shape[0], gk_buf.shape[0]
    here = dq_all.shape[1] // heads
    lanes = heads * here
    past = dk_pad.shape[1] - count * here
    copies = []

    def put(src, dst):
        copy = pltpu.make_async_copy(src, dst, sems.at[len(copies)])
        copy.start()
        copies.append(copy)

    def rows(ref, at):
        return ref[:, at : at + here, :].reshape(count * here, HEAD_DIM)

    for h in range(heads):
        gq_buf[h] = dot3(rows(early, h * here), rows(dq_all, h * here), TN)
        put(gq_buf.at[h], gq_hbm.at[h])
    for g in range(kv):
        for part in range(3):
            gk_buf[g, part * HEAD_DIM : (part + 1) * HEAD_DIM, :] = dot3(
                rows(early, lanes + (g * 3 + part) * here), dk_pad[g, past:, :], TN
            )
        put(gk_buf.at[g], gk_hbm.at[g])
    for copy in copies:
        copy.wait()


def body(count, heads_axis, queries, keys, query_projection, key_projection, offsets, counts):
    rows, width = queries.shape
    here = rows // BLOCK
    heads = width // HEAD_DIM
    kv = keys.shape[1] // HEAD_DIM
    lanes = heads * here
    blocks = REACH * here
    past = blocks - here
    span = heads // kv * BLOCK
    early_rows = lanes + 3 * kv * here
    vmem = pl.BlockSpec(memory_space=pltpu.VMEM)
    hbm = pl.BlockSpec(memory_space=pltpu.HBM)
    dma = pltpu.SemaphoreType.DMA
    passed = 4 * HEAD_DIM * (count * (early_rows + lanes) + kv * (past + count * here))
    early, dq_all, dk_pad, total = pl.pallas_call(
        functools.partial(kernel, count, heads_axis),
        out_shape=(
            pltpu.VMEM((count, early_rows, HEAD_DIM), F32),
            pltpu.VMEM((count, lanes, HEAD_DIM), F32),
            pltpu.VMEM((kv, past + count * here, HEAD_DIM), F32),
            jax.ShapeDtypeStruct((1, 1), F32),
        ),
        in_specs=[hbm] * 6,
        out_specs=(vmem, vmem, vmem, vmem),
        scratch_shapes=[
            pltpu.VMEM(queries.shape, queries.dtype),
            pltpu.VMEM(keys.shape, keys.dtype),
            pltpu.VMEM(query_projection.shape, F32),
            pltpu.VMEM(key_projection.shape, F32),
            pltpu.SMEM(offsets.shape, offsets.dtype),
            pltpu.SMEM((1, here), counts.dtype),
            dma((6,)),
            pltpu.VMEM((past * BLOCK, keys.shape[1]), keys.dtype),
            pltpu.VMEM((count, blocks + 8, lanes), F32),
            pltpu.VMEM((heads_axis, 8, lanes), F32),
            pltpu.VMEM((here * kv, blocks, span), F32),
            pltpu.VMEM((here * kv, blocks, span), F32),
            pltpu.VMEM((here, blocks, 128), F32),
            pltpu.VMEM((blocks, lanes), F32),
            pltpu.VMEM((lanes, HEAD_DIM), F32),
            pltpu.VMEM((count, lanes, HEAD_DIM), F32),
            pltpu.VMEM((kv, past + count * here, HEAD_DIM), F32),
            dma((5, PIECES)),
            dma((REACH - 1, PIECES)),
            dma((count - 1,)),
            dma((count - 1,)),
            dma((count - 1,)),
            dma((count - 1,)),
            dma((heads_axis,)),
            dma((heads_axis,)),
        ],
        compiler_params=pltpu.CompilerParams(
            collective_id=0, has_side_effects=True, vmem_limit_bytes=58 * 1024 * 1024 - passed
        ),
    )(queries, keys, query_projection, key_projection, offsets, counts.reshape(1, here))
    query_gradient, key_gradient = pl.pallas_call(
        finish,
        out_shape=(
            jax.ShapeDtypeStruct(query_projection.shape, F32),
            jax.ShapeDtypeStruct(key_projection.shape, F32),
        ),
        in_specs=[vmem] * 3,
        out_specs=(hbm, hbm),
        scratch_shapes=[
            pltpu.VMEM(query_projection.shape, F32),
            pltpu.VMEM(key_projection.shape, F32),
            dma((heads + kv,)),
        ],
        compiler_params=pltpu.CompilerParams(vmem_limit_bytes=16 * 1024 * 1024),
    )(early, dq_all, dk_pad)
    return query_gradient, key_gradient, total.reshape(())


def solution(mesh):
    placed = (
        P("ctx", "head"),
        P("ctx", "head"),
        P("head", None, None),
        P("head", None, None),
        P("ctx", None),
        P("ctx"),
    )
    return jax.shard_map(
        functools.partial(body, mesh.shape["ctx"], mesh.shape["head"]),
        mesh=mesh,
        in_specs=placed,
        out_specs=(P("head", None, None), P("head", None, None), P()),
        check_vma=False,
    )
```

```python
import functools
import math

import jax
import jax.numpy as jnp
from jax import lax
from jax.experimental import pallas as pl
from jax.experimental.pallas import tpu as pltpu
from jax.sharding import PartitionSpec as P

HEAD_DIM = 128
BLOCK = 64
REACH = 4
PIECES = 2
MESH = pl.DeviceIdType.MESH
F32 = jnp.float32
BF16 = jnp.bfloat16
LOW = -3.0e38
NT = (((1,), (1,)), ((), ()))
NN = (((1,), (0,)), ((), ()))
TN = (((0,), (0,)), ((), ()))


def exact(a, b, dims):
    return lax.dot_general(
        a, b, dims, precision=lax.Precision.HIGHEST, preferred_element_type=F32
    )


def halves(a):
    high = a.astype(BF16)
    return high, (a - high.astype(F32)).astype(BF16)


def dot3(a, b, dims):
    ah, al = halves(a)
    bh, bl = halves(b)
    one = functools.partial(
        lax.dot_general, dimension_numbers=dims, preferred_element_type=F32
    )
    return one(ah, bh) + (one(ah, bl) + one(al, bh))


def flipped(me, mask):
    out = me
    bit = 0
    while mask >> bit:
        if (mask >> bit) & 1:
            size = 1 << bit
            out = out + size - 2 * size * ((me // size) % 2)
        bit += 1
    return out


class Spread:
    def __init__(self, me, count, buf, send, recv):
        self.me, self.buf, self.send, self.recv = me, buf, send, recv
        self.bits = count.bit_length() - 1
        self.index = {}
        for bit in reversed(range(self.bits)):
            for high in range(1 << (self.bits - 1 - bit)):
                self.index[bit, high] = len(self.index)
        self.order = sorted(
            self.index, key=lambda key: (bin(key[1]).count("1"), -key[0])
        )
        self.whole = len(self.order)

    def copy(self, bit, high):
        at = self.index[bit, high]
        slot = flipped(self.me, high << (bit + 1))
        return pltpu.make_async_remote_copy(
            src_ref=self.buf.at[slot],
            dst_ref=self.buf.at[slot],
            send_sem=self.send.at[at],
            recv_sem=self.recv.at[at],
            device_id={"ctx": flipped(self.me, 1 << bit)},
            device_id_type=MESH,
        )

    def start(self):
        for bit in reversed(range(self.bits)):
            self.copy(bit, 0).start()

    def forward(self, begin, end):
        for bit, high in self.order[begin:end]:
            self.copy(bit, high).wait_recv()
            held = (1 << bit) | (high << (bit + 1))
            for lower in reversed(range(bit)):
                self.copy(lower, held >> (lower + 1)).start()

    def finish(self):
        for bit, high in self.order:
            self.copy(bit, high).wait_send()


def kernel(
    count,
    heads_axis,
    q_in,
    k_in,
    wq_in,
    wk_in,
    off_in,
    cnt_in,
    early,
    dq_all,
    dk_pad,
    total_out,
    q_ref,
    k_ref,
    wq_ref,
    wk_ref,
    off_ref,
    cnt_ref,
    load,
    win,
    late,
    peer,
    top,
    mass,
    mask,
    tmap,
    gq_own,
    gq_all,
    gk_pad,
    win_send,
    win_recv,
    early_send,
    early_recv,
    late_send,
    late_recv,
    peer_send,
    peer_recv,
):
    loads = [
        pltpu.make_async_copy(src, dst, load.at[at])
        for at, (src, dst) in enumerate(
            (
                (k_in, k_ref),
                (q_in, q_ref),
                (off_in, off_ref),
                (cnt_in, cnt_ref),
                (wq_in, wq_ref),
                (wk_in, wk_ref),
            )
        )
    ]
    for copy in loads:
        copy.start()
    me = lax.axis_index("ctx")
    side = lax.axis_index("head")
    rows, width = q_ref.shape
    here = rows // BLOCK
    heads = width // HEAD_DIM
    kv = k_ref.shape[1] // HEAD_DIM
    group = heads // kv
    slots = off_ref.shape[1]
    blocks = REACH * here
    past = (REACH - 1) * here
    lanes = heads * here
    bits = count.bit_length() - 1
    span = group * BLOCK

    strip = kv // PIECES * HEAD_DIM
    odd = lax.rem(me, 2) == 1
    even = jnp.logical_not(odd)
    corner = lax.rem(me, 4)

    def lanes_of(at):
        if isinstance(at, int):
            return slice(at * strip, (at + 1) * strip)
        return pl.ds(pl.multiple_of(at * strip, strip), strip)

    def slot_rows(step):
        return pl.ds(pl.multiple_of((REACH - 1 - step) * rows, rows), rows)

    def window_copy(kind, at, held, step, target):
        if held:
            src = win.at[slot_rows(held), lanes_of(at)]
        else:
            src = k_in.at[:, lanes_of(at)]
        return pltpu.make_async_remote_copy(
            src_ref=src,
            dst_ref=win.at[slot_rows(step), lanes_of(at)],
            send_sem=win_send.at[kind, at],
            recv_sem=win_recv.at[step - 1, at],
            device_id={"ctx": lax.rem(target + count, count)},
            device_id_type=MESH,
        )

    def direct_copies(at):
        return (
            (even & (me + 2 < count), window_copy(0, at, 0, 2, me + 2)),
            (even, window_copy(1, at, 0, 1, me + 1)),
            ((corner == 1) & (me + 2 < count), window_copy(2, at, 0, 2, me + 2)),
            (odd & (me + 3 < count), window_copy(3, at, 0, 3, me + 3)),
        )

    def relay_copies(at):
        return (
            (2, even & (me >= 2), window_copy(4, at, 2, 3, me + 1)),
            (2, odd & (me >= 2), window_copy(5, at, 2, 1, me - 1)),
            (3, (corner == 2) & (me >= 3), window_copy(6, at, 3, 2, me - 1)),
        )

    barrier = pltpu.get_barrier_semaphore()
    greeted = 0
    for step in range(1, REACH):
        for other in (lax.rem(me + step, count), lax.rem(me + count - step, count)):
            pl.semaphore_signal(
                barrier, inc=1, device_id={"ctx": other}, device_id_type=MESH
            )
            greeted += 1
    for bit in range(bits):
        pl.semaphore_signal(
            barrier, inc=1, device_id={"ctx": flipped(me, 1 << bit)}, device_id_type=MESH
        )
        greeted += 1
    for step in range(1, heads_axis):
        pl.semaphore_signal(
            barrier,
            inc=1,
            device_id={"head": lax.rem(side + step, heads_axis)},
            device_id_type=MESH,
        )
        greeted += 1
    pl.semaphore_wait(barrier, greeted)

    for at in range(PIECES):
        for condition, copy in direct_copies(at):
            pl.when(condition)(copy.start)

    for step in range(1, REACH):

        @pl.when(me < step)
        def _():
            win[(REACH - 1 - step) * rows : (REACH - step) * rows, :] = jnp.zeros(
                k_ref.shape, k_ref.dtype
            )

    for copy in loads[:4]:
        copy.wait()

    pool_row = lax.broadcasted_iota(jnp.int32, (here, rows), 0)
    pool_col = lax.broadcasted_iota(jnp.int32, (here, rows), 1)
    pool = jnp.where(pool_col // BLOCK == pool_row, 1.0 / BLOCK, 0.0).astype(BF16)
    for h in range(heads):
        early[me, h * here : (h + 1) * here, :] = lax.dot_general(
            pool,
            q_ref[:, h * HEAD_DIM : (h + 1) * HEAD_DIM],
            NN,
            preferred_element_type=F32,
        )
    for g in range(kv):
        keys = k_ref[:, g * HEAD_DIM : (g + 1) * HEAD_DIM]
        split = keys.astype(F32).reshape(here, BLOCK, HEAD_DIM)
        mean = lax.dot_general(pool, keys, NN, preferred_element_type=F32)
        for part, value in enumerate((jnp.max(split, axis=1), jnp.min(split, axis=1), mean)):
            at = lanes + (g * 3 + part) * here
            early[me, at : at + here, :] = value
    first = Spread(me, count, early, early_send, early_recv)

    row_w = lax.broadcasted_iota(jnp.int32, (blocks, 128), 0)
    for j in range(here):
        back = past + j - row_w
        used = jnp.zeros((blocks, 128), F32)
        for c in range(slots):
            off = jnp.where(c < cnt_ref[0, j], off_ref[j, c], -1000)
            used = jnp.where(back == off, 1.0, used)
        mask[j] = jnp.where(row_w >= past - me * here, used, 0.0)

    log_scale = math.log2(math.e) / math.sqrt(HEAD_DIM)
    gap = lax.broadcasted_iota(jnp.int32, (BLOCK, span), 0) - (
        lax.broadcasted_iota(jnp.int32, (BLOCK, span), 1) % BLOCK
    )

    count_row = lax.broadcasted_iota(jnp.int32, (here, rows), 0)
    count_col = lax.broadcasted_iota(jnp.int32, (here, rows), 1)
    tally = jnp.where(count_col // BLOCK == count_row, 1.0, 0.0).astype(BF16)

    def lane(at):
        return pl.ds(pl.multiple_of(at * HEAD_DIM, HEAD_DIM), HEAD_DIM)

    def scored(keys_ref, key_row, j, g, low, high):
        here_rows = slice(j * BLOCK, (j + 1) * BLOCK)
        queries = jnp.concatenate(
            [q_ref[here_rows, lane(g * group + r)] for r in range(group)], axis=0
        )
        keys = keys_ref[pl.ds(key_row + low * BLOCK, (high - low) * BLOCK), lane(g)]
        return lax.dot_general(keys, queries, NT, preferred_element_type=F32)

    def weigh(scores, base, j, g, low, high, diagonal):
        none = [jnp.zeros((1, span), F32)]
        tops, sums = none * low, none * low
        for w in range(low, high):
            part = scores[(w - low) * BLOCK : (w - low + 1) * BLOCK]
            if diagonal and w == j:
                part = jnp.where(gap <= 0, part, LOW)
            best = jnp.max(part, axis=0, keepdims=True)
            tops.append(best)
            power = jnp.exp2((part - best) * log_scale)
            sums.append(jnp.sum(power, axis=0, keepdims=True))
        tops += none * (here - high)
        top[j * kv + g, pl.ds(base, here), :] = jnp.concatenate(tops, axis=0)
        return sums

    def keep(sums, base, j, g, low, high):
        mass[j * kv + g, pl.ds(base, here), :] = jnp.concatenate(
            sums + [jnp.zeros((1, span), F32)] * (here - high), axis=0
        )

    def section(keys_ref, key_row, base, first_g, last_g, bounds, diagonal=False):
        def one(g, carry):
            ahead = scored(keys_ref, key_row, 0, g, *bounds(0))
            for j in range(here):
                scores = ahead
                if j + 1 < here:
                    ahead = scored(keys_ref, key_row, j + 1, g, *bounds(j + 1))
                sums = weigh(scores, base, j, g, *bounds(j), diagonal)
                keep(sums, base, j, g, *bounds(j))
            return carry

        lax.fori_loop(first_g, last_g, one, 0)

    section(k_ref, 0, past, 0, kv, lambda j: (0, j + 1), True)
    loads[4].wait()
    loads[5].wait()
    own_gq = jnp.concatenate(
        [
            exact(early[me, h * here : (h + 1) * here, :], wq_ref[h], NN)
            for h in range(heads)
        ],
        axis=0,
    )
    gq_own[...] = own_gq

    reached = [
        sum(bin(high).count("1") <= ones for _, high in first.order) for ones in range(2)
    ]

    def piece(turn, carry):
        plan = (
            ((3, 0), (2, 0), (3, 1), (1, 0), (2, 1), (1, 1)),
            ((1, 0), (1, 1), (2, 0), (3, 0), (2, 1), (3, 1)),
        )
        step, at = jnp.int32(0), jnp.int32(0)
        for number, (evens, odds) in enumerate(zip(*plan)):
            step = jnp.where(turn == number, jnp.where(odd, odds[0], evens[0]), step)
            at = jnp.where(turn == number, jnp.where(odd, odds[1], evens[1]), at)

        @pl.when(me >= step)
        def _():
            window_copy(0, at, 0, step, me + 2).wait_recv()

        for want, condition, copy in relay_copies(at):
            pl.when(condition & (step == want))(copy.start)

        slot = REACH - 1 - step
        key_row = pl.multiple_of(slot * rows, rows)
        base = pl.multiple_of(slot * here, here)
        each = kv // PIECES

        @pl.when(step == REACH - 1)
        def _():
            section(win, key_row, base, at * each, at * each + each, lambda j: (j, here))

        @pl.when(step < REACH - 1)
        def _():
            section(win, key_row, base, at * each, at * each + each, lambda j: (0, here))

        @pl.when(turn == 1)
        def _():
            first.start()

        return carry

    lax.fori_loop(0, (REACH - 1) * PIECES, piece, 0)
    first.forward(0, reached[0])

    spread_row = lax.broadcasted_iota(jnp.int32, (span, 128), 0)
    spread_col = lax.broadcasted_iota(jnp.int32, (span, 128), 1)
    spread = jnp.where(spread_col == (spread_row // BLOCK) * here, 1.0 / BLOCK, 0.0).astype(BF16)
    tmap[...] = jnp.zeros(tmap.shape, F32)

    def combine(j, carry):
        used = mask[j] > 0.5
        used = jnp.concatenate([used] * (span // 128), axis=1)
        for g in range(kv):
            high = jnp.where(used, top[j * kv + g], LOW)
            best = jnp.max(high, axis=0, keepdims=True)
            share = jnp.where(used, mass[j * kv + g], 0.0) * jnp.exp2((high - best) * log_scale)
            share = share / jnp.sum(share, axis=0, keepdims=True)
            sh, sl = halves(share)
            mean = lax.dot_general(sh, spread, NN, preferred_element_type=F32)
            mean = mean + lax.dot_general(sl, spread, NN, preferred_element_type=F32)
            tmap[...] += pltpu.roll(mean, g * group * here + j, axis=1)
        return carry

    lax.fori_loop(0, here, combine, 0)

    first.forward(reached[0], reached[1])
    win_row = lax.broadcasted_iota(jnp.int32, (past, past * BLOCK), 0)
    win_col = lax.broadcasted_iota(jnp.int32, (past, past * BLOCK), 1)
    win_pool = jnp.where(win_col // BLOCK == win_row, 1.0 / BLOCK, 0.0).astype(BF16)
    near = []
    for g in range(kv):
        keys = win[:, g * HEAD_DIM : (g + 1) * HEAD_DIM]
        split = keys.astype(F32).reshape(past, BLOCK, HEAD_DIM)
        mean = lax.dot_general(win_pool, keys, NN, preferred_element_type=F32)
        acc = None
        for part, value in enumerate((jnp.max(split, axis=1), jnp.min(split, axis=1), mean)):
            at = lanes + (g * 3 + part) * here
            value = jnp.concatenate([value, early[me, at : at + here, :]], axis=0)
            term = exact(value, wk_ref[g, part * HEAD_DIM : (part + 1) * HEAD_DIM, :], NN)
            acc = term if acc is None else acc + term
        near.append(acc)

    def pooled_keys(g, part):
        at = lanes + (g * 3 + part) * here
        return early[:, at : at + here, :].reshape(count * here, HEAD_DIM)

    def window_keys(s):
        at = pl.ds(pl.multiple_of(s * here, here), blocks)
        return jnp.concatenate([gk_pad[g, at, :] for g in range(kv)], axis=0)

    lane = lax.broadcasted_iota(jnp.int32, (blocks, lanes), 1)
    lane_group = lane // (group * here)
    full = exact(jnp.concatenate(near, axis=0), gq_own[...], NT)
    logits = jnp.zeros((blocks, lanes), F32)
    used = jnp.zeros((blocks, lanes), F32)
    for g in range(kv):
        logits = jnp.where(lane_group == g, full[g * blocks : (g + 1) * blocks], logits)
    for j in range(here):
        used = jnp.where(lane % here == j, mask[j], used)
    used = used > 0.5
    logits = jnp.where(used, logits / math.sqrt(HEAD_DIM), LOW)
    logits = logits - jnp.max(logits, axis=0, keepdims=True)
    weights = jnp.where(used, jnp.exp(logits), 0.0)
    norm = jnp.sum(weights, axis=0, keepdims=True)
    log_gate = jnp.where(used, logits - jnp.log(norm), 0.0)
    teacher = jnp.where(used, tmap[...], 0.0)
    log_teacher = jnp.log(jnp.where(teacher > 0.0, teacher, 1.0))
    terms = teacher * (log_teacher - log_gate)
    block_total = count * here
    scale = 1.0 / (math.sqrt(block_total) * math.sqrt(HEAD_DIM))
    slope = jnp.sum(teacher, axis=0, keepdims=True) * (weights / norm) - teacher
    late[me, :blocks, :] = jnp.where(used, slope, 0.0) * scale
    part = terms[:8]
    for at in range(8, blocks, 8):
        part = part + terms[at : at + 8]
    late[me, blocks : blocks + 8, :] = part
    second = Spread(me, count, late, late_send, late_recv)
    second.start()

    first.forward(reached[1], first.whole)
    gk_pad[:, :past, :] = jnp.zeros((kv, past, HEAD_DIM), F32)
    dk_pad[...] = jnp.zeros(dk_pad.shape, F32)
    for g in range(kv):
        acc = exact(pooled_keys(g, 0), wk_ref[g, :HEAD_DIM, :], NN)
        for part in range(1, 3):
            acc = acc + exact(
                pooled_keys(g, part), wk_ref[g, part * HEAD_DIM : (part + 1) * HEAD_DIM, :], NN
            )
        gk_pad[g, past:, :] = acc

    for h in range(heads):
        pooled = early[:, h * here : (h + 1) * here, :].reshape(count * here, HEAD_DIM)
        gq_all[:, h * here : (h + 1) * here, :] = dot3(pooled, wq_ref[h], NN).reshape(
            count, here, HEAD_DIM
        )
        second.forward(h * second.whole // heads, (h + 1) * second.whole // heads)

    total = late[0, blocks : blocks + 8, :]
    for s in range(1, count):
        total = total + late[s, blocks : blocks + 8, :]
    peer[side] = total

    def peer_copy(step):
        return pltpu.make_async_remote_copy(
            src_ref=peer.at[side],
            dst_ref=peer.at[side],
            send_sem=peer_send.at[step - 1],
            recv_sem=peer_recv.at[step - 1],
            device_id={"head": lax.rem(side + step, heads_axis)},
            device_id_type=MESH,
        )

    for step in range(1, heads_axis):
        peer_copy(step).start()

    def backward(s, carry):
        slope = late[s, :blocks, :]
        banded = jnp.concatenate(
            [jnp.where(lane_group == g, slope, 0.0) for g in range(kv)], axis=0
        )
        dq_all[s] = dot3(banded, window_keys(s), TN)
        dk = dot3(banded, gq_all[s], NN)
        at = pl.ds(pl.multiple_of(s * here, here), blocks)
        for g in range(kv):
            dk_pad[g, at, :] += dk[g * blocks : (g + 1) * blocks]
        return carry

    lax.fori_loop(0, count, backward, 0)
    for step in range(1, heads_axis):
        peer_copy(step).wait_recv()
    total = peer[0]
    for step in range(1, heads_axis):
        total = total + peer[step]
    total = jnp.sum(jnp.sum(total, axis=0, keepdims=True), axis=1, keepdims=True)
    total_out[...] = total / (block_total * heads * heads_axis)
    for step in range(1, heads_axis):
        peer_copy(step).wait_send()
    first.finish()
    second.finish()
    for at in range(PIECES):
        for condition, copy in direct_copies(at):
            pl.when(condition)(copy.wait_send)
        for _, condition, copy in relay_copies(at):
            pl.when(condition)(copy.wait_send)


def finish(early, dq_all, dk_pad, gq_hbm, gk_hbm, gq_buf, gk_buf, sems):
    count = early.shape[0]
    heads, kv = gq_buf.shape[0], gk_buf.shape[0]
    here = dq_all.shape[1] // heads
    lanes = heads * here
    past = dk_pad.shape[1] - count * here
    copies = []

    def put(src, dst):
        copy = pltpu.make_async_copy(src, dst, sems.at[len(copies)])
        copy.start()
        copies.append(copy)

    def rows(ref, at):
        return ref[:, at : at + here, :].reshape(count * here, HEAD_DIM)

    for h in range(heads):
        gq_buf[h] = dot3(rows(early, h * here), rows(dq_all, h * here), TN)
        put(gq_buf.at[h], gq_hbm.at[h])
    for g in range(kv):
        for part in range(3):
            gk_buf[g, part * HEAD_DIM : (part + 1) * HEAD_DIM, :] = dot3(
                rows(early, lanes + (g * 3 + part) * here), dk_pad[g, past:, :], TN
            )
        put(gk_buf.at[g], gk_hbm.at[g])
    for copy in copies:
        copy.wait()


def body(count, heads_axis, queries, keys, query_projection, key_projection, offsets, counts):
    rows, width = queries.shape
    here = rows // BLOCK
    heads = width // HEAD_DIM
    kv = keys.shape[1] // HEAD_DIM
    lanes = heads * here
    blocks = REACH * here
    past = blocks - here
    span = heads // kv * BLOCK
    early_rows = lanes + 3 * kv * here
    vmem = pl.BlockSpec(memory_space=pltpu.VMEM)
    hbm = pl.BlockSpec(memory_space=pltpu.HBM)
    dma = pltpu.SemaphoreType.DMA
    passed = 4 * HEAD_DIM * (count * (early_rows + lanes) + kv * (past + count * here))
    early, dq_all, dk_pad, total = pl.pallas_call(
        functools.partial(kernel, count, heads_axis),
        out_shape=(
            pltpu.VMEM((count, early_rows, HEAD_DIM), F32),
            pltpu.VMEM((count, lanes, HEAD_DIM), F32),
            pltpu.VMEM((kv, past + count * here, HEAD_DIM), F32),
            jax.ShapeDtypeStruct((1, 1), F32),
        ),
        in_specs=[hbm] * 6,
        out_specs=(vmem, vmem, vmem, vmem),
        scratch_shapes=[
            pltpu.VMEM(queries.shape, queries.dtype),
            pltpu.VMEM(keys.shape, keys.dtype),
            pltpu.VMEM(query_projection.shape, F32),
            pltpu.VMEM(key_projection.shape, F32),
            pltpu.SMEM(offsets.shape, offsets.dtype),
            pltpu.SMEM((1, here), counts.dtype),
            dma((6,)),
            pltpu.VMEM((past * BLOCK, keys.shape[1]), keys.dtype),
            pltpu.VMEM((count, blocks + 8, lanes), F32),
            pltpu.VMEM((heads_axis, 8, lanes), F32),
            pltpu.VMEM((here * kv, blocks, span), F32),
            pltpu.VMEM((here * kv, blocks, span), F32),
            pltpu.VMEM((here, blocks, 128), F32),
            pltpu.VMEM((blocks, lanes), F32),
            pltpu.VMEM((lanes, HEAD_DIM), F32),
            pltpu.VMEM((count, lanes, HEAD_DIM), F32),
            pltpu.VMEM((kv, past + count * here, HEAD_DIM), F32),
            dma((7, PIECES)),
            dma((REACH - 1, PIECES)),
            dma((count - 1,)),
            dma((count - 1,)),
            dma((count - 1,)),
            dma((count - 1,)),
            dma((heads_axis,)),
            dma((heads_axis,)),
        ],
        compiler_params=pltpu.CompilerParams(
            collective_id=0, has_side_effects=True, vmem_limit_bytes=58 * 1024 * 1024 - passed
        ),
    )(queries, keys, query_projection, key_projection, offsets, counts.reshape(1, here))
    query_gradient, key_gradient = pl.pallas_call(
        finish,
        out_shape=(
            jax.ShapeDtypeStruct(query_projection.shape, F32),
            jax.ShapeDtypeStruct(key_projection.shape, F32),
        ),
        in_specs=[vmem] * 3,
        out_specs=(hbm, hbm),
        scratch_shapes=[
            pltpu.VMEM(query_projection.shape, F32),
            pltpu.VMEM(key_projection.shape, F32),
            dma((heads + kv,)),
        ],
        compiler_params=pltpu.CompilerParams(vmem_limit_bytes=16 * 1024 * 1024),
    )(early, dq_all, dk_pad)
    return query_gradient, key_gradient, total.reshape(())


def solution(mesh):
    placed = (
        P("ctx", "head"),
        P("ctx", "head"),
        P("head", None, None),
        P("head", None, None),
        P("ctx", None),
        P("ctx"),
    )
    return jax.shard_map(
        functools.partial(body, mesh.shape["ctx"], mesh.shape["head"]),
        mesh=mesh,
        in_specs=placed,
        out_specs=(P("head", None, None), P("head", None, None), P()),
        check_vma=False,
    )
```
